32 devices in a mesh: row: 4 (over y, core), col: 8 (over z, x).
Axes of the slice: x: 2, y: 2, z: 4, core: 2. Of those that a mesh axis runs over, the one named last changes fastest.
Arguments:
- hess_inv: float32 [16384, 16384], P('row', 'col'), as said below
- weights: bfloat16 [6144, 16384], P('row', 'col'), may hold values from -6 to 6
- removed: int32 [128], replicated, may hold values from 0 to 16383, as said below
Outputs:
- hess_out: float32 [16384, 16384], P('row', 'col')
- weight_out: bfloat16 [6144, 16384], P('row', 'col')
The draws below stay inside these ranges and needn't reach their ends.
Inputs may be any that keep to these rules, and one draw needn't show every extreme that they name: `removed`: sorted ascending and distinct; each aligned block of 2048 columns holds at most 48 of them, and at least one block holds exactly 48. `hess_inv`: symmetric and positive definite.
All inputs are finite; a program needn't handle non-finite values.
Results may differ from the reference program's by a relative error of at most 0.005.
Values may be sent and summed in bfloat16 or wider, within the bound.
No kernel may reach another device: no remote copies, remote signals or barrier semaphores. Data moves between devices by JAX's collectives and lax.ppermute only.
A program may use at most 128 MiB of HBM per device.

```python
import math
import jax
import jax.numpy as jnp
from jax import lax

N = 16384
ROWS = 6144
TILE = 2048
REMOVED = 128
MOST = 48


def draw_hess_inv(key, part):
    first_key, second_key, third_key, fourth_key = jax.random.split(jax.random.fold_in(key, 202), 4)
    factor_rank = 768
    noise_part = jax.random.normal(first_key, (N, N), jnp.float32)
    factor_part = jax.random.normal(third_key, (N, factor_rank), jnp.float32)
    diag_part = jax.random.uniform(second_key, (N,), jnp.float32, 1.5, 3.0)
    strength = 48.0
    log_reach = math.log(16.0)
    weight_mean = 46.0
    amplitude = jnp.exp(jax.random.uniform(fourth_key, (factor_rank,), jnp.float32, 0.0, log_reach))
    scaled_part = factor_part * amplitude[None, :]
    symmetric = (noise_part + noise_part.T) * (0.3536 / math.sqrt(N))
    shared = jnp.dot(scaled_part, scaled_part.T, precision=lax.Precision.HIGHEST) * (strength / (factor_rank * weight_mean))
    position = jnp.arange(N)
    return (symmetric + shared).at[position, position].add(diag_part)


def draw_removed(key, part):
    base_key = jax.random.fold_in(key, 101)
    first_key, second_key, third_key, fourth_key = jax.random.split(base_key, 4)
    tile_total = N // TILE
    full_tile = jax.random.randint(first_key, (), 0, tile_total)
    tile_caps = jax.random.randint(second_key, (tile_total,), MOST // 2, MOST + 1)
    tile_caps = jnp.where(jnp.arange(tile_total) == full_tile, 0, tile_caps)
    slot_tile = jnp.repeat(jnp.arange(tile_total), MOST)
    slot_rank = jnp.tile(jnp.arange(MOST), tile_total)
    usable = slot_rank < tile_caps[slot_tile]
    slot_score = jax.random.permutation(third_key, tile_total * MOST)
    slot_score = jnp.where(usable, slot_score, slot_score + tile_total * MOST)
    picked = jnp.argsort(slot_score)[:REMOVED - MOST]
    tile_keys = jax.random.split(fourth_key, tile_total)
    col_perms = jax.vmap(lambda inner: jax.random.permutation(inner, TILE))(tile_keys)
    full_cols = full_tile * TILE + col_perms[full_tile, :MOST]
    other_cols = slot_tile[picked] * TILE + col_perms[slot_tile[picked], slot_rank[picked]]
    return jnp.sort(jnp.concatenate([full_cols, other_cols])).astype(jnp.int32)


def block_levels(key, dims, cuts, least, largest):
    loudness = 1.0
    for dim, blocks in cuts:
        draws = jax.random.uniform(jax.random.fold_in(jax.random.fold_in(key, 6), dim), (blocks,), jnp.float32, least / len(cuts), largest / len(cuts))
        loudness = loudness * jnp.repeat(jnp.exp(draws), dims[dim] // blocks).reshape((-1,) + (1,) * (len(dims) - 1 - dim))
    return loudness


def noise(own_key, dims, spread, reach, shards=(), kind=jnp.bfloat16):
    drawn = jax.random.normal(own_key, dims, jnp.float32) * spread
    if len(shards) > 0:
        drawn = block_levels(own_key, dims, shards, -0.22, 0.18) * drawn
    return jnp.clip(drawn, min=-reach, max=reach).astype(kind)


def setup_inputs(seed: int = 0) -> dict:
    arg_keys = jax.random.split(jax.random.key(seed), 4)
    return {
        "hess_inv": draw_hess_inv(jax.random.fold_in(arg_keys[3], 71), 0),
        "weights": noise(arg_keys[1], (ROWS, N), 1.0, 6.0, ((0, 4), (1, 8))),
        "removed": draw_removed(jax.random.fold_in(arg_keys[3], 71), 0),
    }


def reference(hess_inv, weights, removed):
    block_rows = jnp.take(hess_inv, removed, axis=0)
    removed_block = jnp.take(block_rows, removed, axis=1)
    factor = jnp.linalg.cholesky(removed_block)
    identity = jnp.eye(removed_block.shape[0], dtype=jnp.float32)
    factor_inv = jax.scipy.linalg.solve_triangular(factor, identity, lower=True)
    block_inv = jnp.dot(factor_inv.T, factor_inv, precision=lax.Precision.HIGHEST)
    coupling = jnp.dot(block_inv, block_rows, precision=lax.Precision.HIGHEST)
    hess_cols = jnp.take(hess_inv, removed, axis=1)
    hess_out = hess_inv - jnp.dot(hess_cols, coupling, precision=lax.Precision.HIGHEST)
    weight_cols = jnp.take(weights, removed, axis=1).astype(jnp.float32)
    weight_out = (weights.astype(jnp.float32) - jnp.dot(weight_cols, coupling, precision=lax.Precision.HIGHEST)).astype(jnp.bfloat16)
    return (hess_out, weight_out)
```

```python
import functools

import jax
import jax.numpy as jnp
from jax import lax
from jax.experimental import pallas as pl
from jax.experimental.pallas import tpu as pltpu
from jax.sharding import PartitionSpec as P

MOST = 48
F32 = jnp.float32
BF16 = jnp.bfloat16


def spread(block, axis, owner):
    block = jnp.where(lax.axis_index(axis) == owner, block, jnp.zeros_like(block))
    return lax.psum(block, axis)


def pick_owned(source, removed, tile_index, tile_size, slot_count, which_axis):
    before = jnp.sum((removed < tile_index * tile_size).astype(jnp.int32))
    within = jnp.sum((removed // tile_size == tile_index).astype(jnp.int32))
    slot_rank = jnp.arange(slot_count, dtype=jnp.int32)
    chosen = jnp.clip(before + slot_rank, 0, removed.shape[0] - 1)
    local_col = jnp.clip(removed[chosen] - tile_index * tile_size, 0, tile_size - 1)
    taken_part = jnp.take(source, local_col, axis=which_axis)
    live_slot = slot_rank < within
    mask_shape = [1, 1]
    mask_shape[which_axis] = slot_count
    return jnp.where(live_slot.reshape(mask_shape), taken_part, jnp.zeros((), taken_part.dtype))


def slot_map(removed, tile_size, slot_count):
    which_tile = removed // tile_size
    first_pos = jnp.sum(
        (removed[None, :] < (which_tile * tile_size)[:, None]).astype(jnp.int32), axis=1
    )
    position = jnp.arange(removed.shape[0], dtype=jnp.int32)
    return which_tile * slot_count + position - first_pos


def general(hess_inv, weights, removed):
    row_count = lax.axis_size("row")
    col_count = lax.axis_size("col")
    row_index = lax.axis_index("row")
    col_index = lax.axis_index("col")
    row_tile, col_tile = hess_inv.shape
    tile_ratio = col_count // row_count
    col_slots = slot_map(removed, col_tile, MOST)
    packed_weight = pick_owned(weights, removed, col_index, col_tile, MOST, 1)
    packed_rows = pick_owned(hess_inv, removed, row_index, row_tile, tile_ratio * MOST, 0)
    gathered = lax.all_gather(packed_rows, "row", axis=0, tiled=True)
    upper_rows = jnp.take(gathered, slot_map(removed, row_tile, tile_ratio * MOST), axis=0)
    pieces = [
        spread(upper_rows.astype(BF16), "col", row_index * tile_ratio + offset).astype(F32)
        for offset in range(tile_ratio)
    ]
    left_rows = jnp.concatenate(pieces, axis=1)
    weight_wide = lax.all_gather(packed_weight, "col", axis=1, tiled=True)
    weight_left = jnp.take(weight_wide, col_slots, axis=1)
    own_cols = pick_owned(upper_rows, removed, col_index, col_tile, MOST, 1)
    block_wide = lax.all_gather(own_cols, "col", axis=1, tiled=True)
    removed_block = jnp.take(block_wide, col_slots, axis=1)
    factor = jnp.linalg.cholesky(removed_block)
    identity = jnp.eye(removed_block.shape[0], dtype=F32)
    factor_inv = jax.scipy.linalg.solve_triangular(factor, identity, lower=True)
    block_inv = jnp.dot(factor_inv.T, factor_inv, precision=lax.Precision.HIGHEST)
    coupling = jnp.dot(block_inv, upper_rows, precision=lax.Precision.HIGHEST)
    correction = lax.dot_general(
        left_rows, coupling, (((0,), (0,)), ((), ())), precision=lax.Precision.HIGHEST
    )
    hess_out = hess_inv - correction
    weight_fix = jnp.dot(weight_left.astype(F32), coupling, precision=lax.Precision.HIGHEST)
    weight_out = (weights.astype(F32) - weight_fix).astype(BF16)
    return (hess_out, weight_out)


def split3(x):
    hi = x.astype(BF16)
    rest = x - hi.astype(F32)
    mid = rest.astype(BF16)
    lo = (rest - mid.astype(F32)).astype(BF16)
    return hi, mid, lo


def dot(a, b):
    return jnp.dot(a, b, preferred_element_type=F32)


def pick_rows_kernel(rem_ref, info_ref, remv_ref, hess_ref, keep_ref, send_ref, rows_ref, tiles_ref, sems):
    slots, cols = rows_ref.shape
    row_tile = hess_ref.shape[0]
    half = cols // 2
    first_row, first_col, core = info_ref[0], info_ref[1], info_ref[2]

    def owned(i):
        return jnp.logical_and(rem_ref[i] >= first_row, rem_ref[i] < first_row + row_tile)

    def copy(i):
        row = lax.clamp(0, rem_ref[i] - first_row, row_tile - 1)
        at = pl.multiple_of((row // 8) * 8, 8)
        return pltpu.make_async_copy(hess_ref.at[pl.ds(at, 8), :], tiles_ref.at[i], sems.at[i])

    def start(i, _):
        pl.when(owned(i))(lambda: copy(i).start())
        return 0

    lax.fori_loop(0, slots, start, 0)
    rows_ref[...] = jnp.zeros_like(rows_ref)

    def take(i, _):
        @pl.when(owned(i))
        def _():
            copy(i).wait()
            rows_ref[pl.ds(i, 1), :] = tiles_ref[i, pl.ds(lax.rem(rem_ref[i] - first_row, 8), 1), :]

        return 0

    lax.fori_loop(0, slots, take, 0)
    at_col = lax.broadcasted_iota(jnp.int32, (cols, slots), 0) + first_col
    onehot = jnp.where(at_col == remv_ref[...], 1.0, 0.0).astype(BF16)
    for n, part in enumerate(split3(rows_ref[...])):
        picked = dot(part, onehot).astype(BF16)
        keep_ref[:, half + n * slots : half + (n + 1) * slots] = picked
        send_ref[:, half + n * slots : half + (n + 1) * slots] = picked
    keep_ref[:, :half] = rows_ref[:, pl.ds(pl.multiple_of(core * half, half), half)].astype(BF16)
    send_ref[:, :half] = rows_ref[:, pl.ds(pl.multiple_of((1 - core) * half, half), half)].astype(BF16)


def pick_rows(removed, info, hess_inv):
    slots = removed.shape[0]
    cols = hess_inv.shape[1]
    shape = jax.ShapeDtypeStruct((slots, cols // 2 + 3 * slots), BF16)
    return pl.pallas_call(
        pick_rows_kernel,
        name="pick_rows",
        out_shape=(shape, shape),
        grid_spec=pltpu.PrefetchScalarGridSpec(
            num_scalar_prefetch=2,
            grid=(),
            in_specs=[pl.BlockSpec(memory_space=pltpu.VMEM), pl.BlockSpec(memory_space=pl.ANY)],
            out_specs=[pl.BlockSpec(memory_space=pltpu.VMEM)] * 2,
            scratch_shapes=[
                pltpu.VMEM((slots, cols), F32),
                pltpu.VMEM((slots, 8, cols), F32),
                pltpu.SemaphoreType.DMA((slots,)),
            ],
        ),
    )(removed, info, removed[None, :], hess_inv)


def pick_weights_kernel(info_ref, remv_ref, w_ref, keep_ref, send_ref, onehot_ref):
    step = pl.program_id(0)
    cols, slots = onehot_ref.shape

    @pl.when(step == 0)
    def _():
        at_col = lax.broadcasted_iota(jnp.int32, (cols, slots), 0) + info_ref[1]
        onehot_ref[...] = jnp.where(at_col == remv_ref[...], 1.0, 0.0).astype(BF16)

    picked = dot(w_ref[...], onehot_ref[...]).astype(BF16)
    half = pl.num_programs(0) // 2

    @pl.when(step < half)
    def _():
        send_ref[...] = picked

    @pl.when(step >= half)
    def _():
        keep_ref[...] = picked


def pick_weights(info, removed, weights, block):
    rows, cols = weights.shape
    slots = removed.shape[0]
    half = rows // 2 // block
    shape = jax.ShapeDtypeStruct((rows // 2, slots), BF16)

    def in_map(i, info_ref):
        side = jnp.where(i < half, 1 - info_ref[3], info_ref[3])
        return (side * half + lax.rem(i, half), 0)

    return pl.pallas_call(
        pick_weights_kernel,
        name="pick_weights",
        out_shape=(shape, shape),
        grid_spec=pltpu.PrefetchScalarGridSpec(
            num_scalar_prefetch=1,
            grid=(2 * half,),
            in_specs=[pl.BlockSpec((1, slots), lambda i, s: (0, 0)), pl.BlockSpec((block, cols), in_map)],
            out_specs=[
                pl.BlockSpec((block, slots), lambda i, s: (jnp.maximum(i - half, 0), 0)),
                pl.BlockSpec((block, slots), lambda i, s: (jnp.minimum(i, half - 1), 0)),
            ],
            scratch_shapes=[pltpu.VMEM((cols, slots), BF16)],
        ),
    )(info, removed[None, :], weights)


def couple_kernel(info_ref, block_ref, own_ref, other_ref, out_ref, a_ref):
    n = block_ref.shape[0]
    half = own_ref.shape[1]
    a = block_ref[...]
    lane = lax.broadcasted_iota(jnp.int32, (n, n), 1)
    sub = lax.broadcasted_iota(jnp.int32, (n, n), 0)
    for k in range(n):
        pivot = 1.0 / a[k : k + 1, k : k + 1]
        scaled = a[k : k + 1, :] * pivot
        scaled = jnp.where(lane[:1] == k, pivot, scaled)
        column = a[:, k : k + 1]
        cleared = jnp.where(lane == k, 0.0, a) - column * scaled
        a = jnp.where(sub == k, scaled, cleared)
    parts = split3(a)
    for source, place in ((own_ref, info_ref[2]), (other_ref, 1 - info_ref[2])):
        t = source[...]
        k_half = dot(parts[0], t) + (dot(parts[1], t) + dot(parts[2], t))
        hi = k_half.astype(BF16)
        lo = (k_half - hi.astype(F32)).astype(BF16)
        at = pl.ds(pl.multiple_of(place * half, half), half)
        out_ref[:n, at] = hi
        out_ref[n:, at] = lo


def couple(info, block, own, other):
    n, half = own.shape
    return pl.pallas_call(
        couple_kernel,
        name="couple",
        out_shape=jax.ShapeDtypeStruct((2 * n, 2 * half), BF16),
        in_specs=[pl.BlockSpec(memory_space=pltpu.SMEM)] + [pl.BlockSpec(memory_space=pltpu.VMEM)] * 3,
        out_specs=pl.BlockSpec(memory_space=pltpu.VMEM),
        scratch_shapes=[pltpu.VMEM((n, n), F32)],
    )(info, block, own, other)


def update_hess_kernel(off_ref, hess_ref, left_ref, k_ref, *rest):
    out_ref = rest[-1]
    left = left_ref[...]
    left = jnp.concatenate([left, left], axis=0)
    fix = lax.dot_general(left, k_ref[...], (((0,), (0,)), ((), ())), preferred_element_type=F32)
    out_ref[...] = hess_ref[...] - fix


def update_hess(offset, hess_inv, left, k2, prev, block):
    rows, cols = hess_inv.shape
    slots, count = left.shape
    here = pl.BlockSpec((block, cols), lambda i, off: (off[0] + i, 0))
    in_specs = [
        here,
        pl.BlockSpec((slots, block), lambda i, off: (0, i)),
        pl.BlockSpec(k2.shape, lambda i, off: (0, 0)),
    ]
    args = [offset, hess_inv, left, k2]
    aliases = {}
    if prev is not None:
        in_specs.append(pl.BlockSpec(memory_space=pl.ANY))
        args.append(prev)
        aliases = {4: 0}
    return pl.pallas_call(
        update_hess_kernel,
        name="update_hess",
        out_shape=jax.ShapeDtypeStruct((rows, cols), F32),
        grid_spec=pltpu.PrefetchScalarGridSpec(
            num_scalar_prefetch=1, grid=(count // block,), in_specs=in_specs, out_specs=here
        ),
        input_output_aliases=aliases,
        cost_estimate=pl.CostEstimate(
            flops=4 * count * cols * slots, bytes_accessed=8 * count * cols, transcendentals=0
        ),
    )(*args)


def update_weights_kernel(info_ref, w_ref, own_ref, other_ref, k_ref, out_ref):
    step = pl.program_id(0)
    half = pl.num_programs(0) // 2
    block = w_ref.shape[0]
    at = pl.ds(pl.multiple_of(lax.rem(step, half) * block, block), block)
    left = jnp.where(step < half, own_ref[at, :], other_ref[at, :])
    left = jnp.concatenate([left, left], axis=1)
    out_ref[...] = (w_ref[...].astype(F32) - dot(left, k_ref[...])).astype(BF16)


def update_weights(info, weights, own, other, k2, block):
    rows, cols = weights.shape
    half = rows // 2 // block

    def here(i, info_ref):
        side = jnp.where(i < half, info_ref[3], 1 - info_ref[3])
        return (side * half + lax.rem(i, half), 0)

    whole = lambda a: pl.BlockSpec(a.shape, lambda i, s: (0, 0))
    return pl.pallas_call(
        update_weights_kernel,
        name="update_weights",
        out_shape=jax.ShapeDtypeStruct((rows, cols), BF16),
        grid_spec=pltpu.PrefetchScalarGridSpec(
            num_scalar_prefetch=1,
            grid=(2 * half,),
            in_specs=[pl.BlockSpec((block, cols), here), whole(own), whole(other), whole(k2)],
            out_specs=pl.BlockSpec((block, cols), here),
        ),
        cost_estimate=pl.CostEstimate(
            flops=4 * rows * cols * k2.shape[0] // 2, bytes_accessed=4 * rows * cols, transcendentals=0
        ),
    )(info, weights, own, other, k2)


HOLDER = (
    ((0, 3, 1, 2), (2, 1, 0, 3), (0, 3, 2, 1), (1, 2, 0, 3)),
    ((1, 2, 0, 3), (3, 0, 1, 2), (1, 2, 3, 0), (0, 3, 1, 2)),
)


def fast(hess_inv, weights, removed):
    rows_n, cols_n = lax.axis_size("row"), lax.axis_size("col")
    row, col = lax.axis_index("row"), lax.axis_index("col")
    row_tile, col_tile = hess_inv.shape
    ratio = cols_n // rows_n
    slots = removed.shape[0]
    half = col_tile // 2
    x, z = lax.rem(col, ratio), col // ratio
    core = lax.rem(row, 2)

    def swap(value, axis, bit):
        n = rows_n if axis == "row" else cols_n
        return lax.ppermute(value, axis, [(i, i ^ bit) for i in range(n)])

    block = 128
    waves = []
    for table in HOLDER:
        held = sum(
            jnp.where(jnp.logical_and(row == r, z == w), table[r][w] % 2, 0)
            for r in range(rows_n)
            for w in range(rows_n)
        )
        waves.append(held)
    per = half // block
    offsets = [(xx * 2 + h) * per for h in waves for xx in (x, 1 - x)]
    info = jnp.stack([row * row_tile, col * col_tile, core, x, *offsets]).astype(jnp.int32)

    keep, send = pick_rows(removed, info, hess_inv)
    merged = keep + swap(send, "row", 1)
    w_keep, w_send = pick_weights(info, removed, weights, 256)
    merged = merged + swap(merged, "row", 2)
    own = merged[:, :half]

    pieces = [merged[:, half + n * slots : half + (n + 1) * slots].astype(F32) for n in range(3)]
    removed_block = pieces[0] + pieces[1] + pieces[2]
    for bit in (1, 2, 4):
        removed_block = removed_block + swap(removed_block, "col", bit)
    other = swap(own, "row", 1)
    k2 = couple(info, removed_block, own, other)

    lefts = []
    for table in HOLDER:
        pairs = [
            (table[r][w] * cols_n + r * ratio + xx, r * cols_n + w * ratio + xx)
            for r in range(rows_n)
            for w in range(rows_n)
            for xx in range(ratio)
        ]
        piece = lax.ppermute(own, ("row", "col"), pairs)
        lefts.append(piece)
        lefts.append(swap(piece, "col", 1))

    w_part = w_keep + swap(w_send, "col", 1)
    for bit in (2, 4):
        w_part = w_part + swap(w_part, "col", bit)
    w_other = swap(w_part, "col", 1)

    weight_out = update_weights(info, weights, w_part, w_other, k2, 256)
    hess_out = None
    for n in (0, 2, 1, 3):
        hess_out = update_hess(info[4 + n : 5 + n], hess_inv, lefts[n], k2, hess_out, block)
    return (hess_out, weight_out)


def on_device(hess_inv, weights, removed):
    fits = (
        lax.axis_size("row") == len(HOLDER[0])
        and lax.axis_size("col") == 2 * lax.axis_size("row")
        and hess_inv.shape[1] % 256 == 0
        and weights.shape[0] % 512 == 0
        and removed.shape[0] == 128
    )
    return (fast if fits else general)(hess_inv, weights, removed)


def solution(mesh):
    placed = (P("row", "col"), P("row", "col"), P())
    return jax.shard_map(
        on_device,
        mesh=mesh,
        in_specs=placed,
        out_specs=(P("row", "col"), P("row", "col")),
        check_vma=False,
    )
```
